32 devices in a mesh: grp: 2 (over x), ctx: 4 (over y, core), head: 4 (over z).
Axes of the slice: x: 2, y: 2, z: 4, core: 2. Of those that a mesh axis runs over, the one named last changes fastest.
Arguments:
- queries: bfloat16 [8192, 64, 128], P(('grp', 'ctx'), 'head'), parts along dimension 0, may hold values from -8 to 8
- keys: bfloat16 [8192, 4, 128], P(('grp', 'ctx')), parts along dimension 0, may hold values from -8 to 8
- values: bfloat16 [8192, 4, 128], P(('grp', 'ctx')), parts along dimension 0, may hold values from -6 to 6
- compress_weight: float32 [2, 32, 128], replicated, may hold values from 0.1 to 0.4
- gate_weight: bfloat16 [3, 64, 128], P(None, 'head'), may hold values from -0.5 to 0.5
- selection: int32 [128, 4, 16], P('grp'), parts along dimension 0, may hold values from 0 to 63, as said below
- seq_len: int32 [2], P('grp'), parts along dimension 0, may hold values from 2048 to 4096
Outputs:
- attended: bfloat16 [8192, 64, 128], P(('grp', 'ctx'), 'head'), parts along dimension 0
The draws below stay inside these ranges and needn't reach their ends.
There are 2 independent parts, one for each index of `grp`. The reference program is written for one: setup_inputs(seed, part) draws one part's arguments, and reference() takes and returns one part's arrays. A program takes and returns all parts, laid end to end along the dimension named above; an argument that names none is the same for every part. Nothing has to cross between parts.
Inputs may be any that keep to these rules, and one draw needn't show every extreme that they name: `selection`: each row holds 16 distinct block indices in increasing order, always including its own query block b, and b - 1 when that block lies on the same index of ctx. Every selected block that lies on another index of ctx lies on an earlier one. For one group, the distinct blocks of one index of ctx selected by all query blocks of a later index number exactly 4.
All inputs are finite; a program needn't handle non-finite values.
Results may differ from the reference program's by a relative error of at most 0.005.
Values may be sent and summed in bfloat16 or wider, within the bound.
A program may use at most 256 MiB of HBM per device.

```python
import math
import jax
import jax.numpy as jnp
from jax import lax

H = 64
G = 4
DH = 128
STRIDE = 16
SBLK = 64
NSEL = 16
WIN = 512
TOKENS_PER_SHARD = 1024
CBLK = 32
TOKENS = 4096
NQB = 64
CAP = 4


def draw_queries(key, part):
    noise = jax.random.normal(jax.random.fold_in(key, 1), (TOKENS, H, DH), jnp.float32)
    field = noise
    return jnp.clip(field, -8.0, 8.0).astype(jnp.bfloat16)


def draw_keys(key, part):
    noise = jax.random.normal(jax.random.fold_in(key, 3), (TOKENS, G, DH), jnp.float32)
    field = noise
    return jnp.clip(field, -8.0, 8.0).astype(jnp.bfloat16)


def draw_selection(key, part):
    device_count = TOKENS // TOKENS_PER_SHARD
    per_device = TOKENS_PER_SHARD // SBLK
    block_total = TOKENS // SBLK
    random_rank = jax.random.randint(jax.random.fold_in(key, 5), (device_count, device_count, G, per_device), 0, 4096)
    _, picked = lax.top_k(random_rank * per_device + jnp.arange(per_device), CAP)
    source = jnp.arange(device_count)[None, :, None, None]
    target = jnp.arange(device_count)[:, None, None, None]
    global_ids = source * per_device + picked
    slot_value = (source * CAP + jnp.arange(CAP)) % per_device
    alive = source < target
    block_ids = jnp.arange(block_total)
    matches = (global_ids[..., None] == block_ids) & alive[..., None]
    in_pool = jnp.any(matches, axis=(1, 3))
    forced_slot = jnp.max(jnp.where(matches, slot_value[..., None], -1), axis=(1, 3))
    query_dev = block_ids // per_device
    query_local = block_ids % per_device
    pool_rows = in_pool[query_dev]
    forced_rows = forced_slot[query_dev] == query_local[:, None, None]
    own_dev = block_ids[None, :] // per_device == query_dev[:, None]
    causal = block_ids[None, :] <= block_ids[:, None]
    nearest = (block_ids[None, :] == block_ids[:, None]) | (block_ids[None, :] == block_ids[:, None] - 1) & own_dev
    tier = jnp.where(forced_rows & pool_rows, 4, jnp.where(nearest[:, None, :], 3, jnp.where(pool_rows | (own_dev & causal)[:, None, :], 2, jnp.where(own_dev[:, None, :], 1, 0))))
    jitter = jax.random.randint(jax.random.fold_in(key, 6), (block_total, G, block_total), 0, 4096)
    ranking = tier * 16777216 + jitter * 2048 + block_ids
    _, chosen = lax.top_k(ranking, NSEL)
    return jnp.sort(chosen, axis=-1).astype(jnp.int32)


def block_levels(own_key, shape, shards, low, top_value):
    factor_of = 1.0
    for axis_at, shards_of in shards:
        draws = jax.random.uniform(jax.random.fold_in(jax.random.fold_in(own_key, 6), axis_at), (shards_of,), jnp.float32, low / len(shards), top_value / len(shards))
        factor_of = factor_of * jnp.repeat(jnp.exp(draws), shape[axis_at] // shards_of).reshape((-1,) + (1,) * (len(shape) - 1 - axis_at))
    return factor_of


def scatter_about(key, dims, scale, most, split=(), kind=jnp.bfloat16):
    level = block_levels(key, dims, split, -0.22, 0.18) if split else 1.0
    values = jax.random.normal(key, dims, jnp.float32) * scale * level
    return jnp.minimum(jnp.maximum(values, -most), most).astype(kind)


def setup_inputs(seed: int = 0, part: int = 0) -> dict:
    key_of = jax.random.split(jax.random.key(seed), 8)
    part_splits = jax.random.split(jax.random.fold_in(key_of[7], part), 8)
    queries = draw_queries(jax.random.fold_in(jax.random.fold_in(key_of[7], part), 71), part)
    keys = draw_keys(jax.random.fold_in(jax.random.fold_in(key_of[7], part), 71), part)
    values = scatter_about(part_splits[2], (TOKENS, G, DH), 1.0, 6.0, ((0, 4),))
    compress_weight = jnp.clip(jnp.exp(jax.random.uniform(key_of[3], (2, CBLK, DH), jnp.float32, math.log(0.1), math.log(0.4))), 0.1, 0.4)
    gate_weight = scatter_about(key_of[4], (3, H, DH), DH ** -0.5, 0.5, ((1, 4),))
    selection = draw_selection(jax.random.fold_in(jax.random.fold_in(key_of[7], part), 71), part)
    seq_len = jax.random.randint(part_splits[6], (1,), TOKENS // 2, TOKENS + 1).astype(jnp.int32)
    return {"queries": queries, "keys": keys, "values": values, "compress_weight": compress_weight, "gate_weight": gate_weight, "selection": selection, "seq_len": seq_len}


NEGATIVE = -1e+30

def branch_softmax(scores, visible, vals):
    masked = jnp.where(visible, scores, NEGATIVE)
    largest = lax.optimization_barrier(jnp.max(masked, axis=-1, keepdims=True))
    weights = jnp.where(visible, jnp.exp(masked - largest), 0.0)
    weight_sum = lax.optimization_barrier(jnp.sum(weights, axis=-1))
    rounded = lax.optimization_barrier(weights.astype(jnp.bfloat16)).astype(jnp.float32)
    mixed = jnp.einsum('tgjk,gkd->tgjd', rounded, vals.astype(jnp.float32), precision=lax.Precision.HIGHEST)
    return mixed / jnp.maximum(weight_sum, 1.0)[..., None]

def compress(field, weight):
    widened = field.astype(jnp.float32)
    comp_count = TOKENS // STRIDE
    leading = jnp.concatenate([jnp.zeros((STRIDE, G, DH), jnp.float32), widened[:TOKENS - STRIDE]], axis=0)
    leading = leading.reshape(comp_count, STRIDE, G, DH)
    behind = widened.reshape(comp_count, STRIDE, G, DH)
    first_sum = lax.optimization_barrier(jnp.sum(leading * weight[None, :STRIDE, None, :], axis=1))
    second_sum = lax.optimization_barrier(jnp.sum(behind * weight[None, STRIDE:, None, :], axis=1))
    return (first_sum + second_sum).astype(jnp.bfloat16)

def reference(queries, keys, values, compress_weight, gate_weight, selection, seq_len):
    group_heads = H // G
    score_scale = 1.0 / math.sqrt(DH)
    comp_keys = compress(keys, compress_weight[0]).astype(jnp.float32)
    comp_values = jnp.transpose(compress(values, compress_weight[1]), (1, 0, 2))
    comp_count = TOKENS // STRIDE
    comp_end = jnp.arange(comp_count) * STRIDE + STRIDE - 1
    padded_keys = jnp.concatenate([jnp.zeros((WIN, G, DH), jnp.bfloat16), keys], axis=0)
    padded_values = jnp.concatenate([jnp.zeros((WIN, G, DH), jnp.bfloat16), values], axis=0)
    block_keys = jnp.transpose(keys.reshape(NQB, SBLK, G, DH), (2, 0, 1, 3))
    block_values = jnp.transpose(values.reshape(NQB, SBLK, G, DH), (2, 0, 1, 3))
    gate_wide = gate_weight.astype(jnp.float32)
    group_ids = jnp.arange(G)[:, None]

    def one_block(block_index):
        start_at = block_index * SBLK
        query_portion = lax.dynamic_slice_in_dim(queries, start_at, SBLK, 0).astype(jnp.float32)
        query_groups = query_portion.reshape(SBLK, G, group_heads, DH)
        token_pos = start_at + jnp.arange(SBLK)
        scores = jnp.einsum('tgjd,kgd->tgjk', query_groups, comp_keys, precision=lax.Precision.HIGHEST) * score_scale
        visible = (comp_end[None, :] <= token_pos[:, None])[:, None, None, :]
        compressed_out = branch_softmax(scores, visible, comp_values)
        sliding_keys = lax.dynamic_slice_in_dim(padded_keys, start_at, WIN + SBLK, 0).astype(jnp.float32)
        window_values = jnp.transpose(lax.dynamic_slice_in_dim(padded_values, start_at, WIN + SBLK, 0), (1, 0, 2))
        key_pos = start_at - WIN + jnp.arange(WIN + SBLK)
        visible = (key_pos[None, :] <= token_pos[:, None]) & (key_pos[None, :] > token_pos[:, None] - WIN) & (key_pos[None, :] >= 0)
        scores = jnp.einsum('tgjd,kgd->tgjk', query_groups, sliding_keys, precision=lax.Precision.HIGHEST) * score_scale
        window_out = branch_softmax(scores, visible[:, None, None, :], window_values)
        picked = selection[block_index]
        chosen_keys = block_keys[group_ids, picked].reshape(G, NSEL * SBLK, DH).astype(jnp.float32)
        chosen_values = block_values[group_ids, picked].reshape(G, NSEL * SBLK, DH)
        chosen_pos = (picked[:, :, None] * SBLK + jnp.arange(SBLK)).reshape(G, NSEL * SBLK)
        visible = (chosen_pos[None, :, :] <= token_pos[:, None, None])[:, :, None, :]
        scores = jnp.einsum('tgjd,gkd->tgjk', query_groups, chosen_keys, precision=lax.Precision.HIGHEST) * score_scale
        selected_out = branch_softmax(scores, visible, chosen_values)
        gate_values = jax.nn.sigmoid(jnp.einsum('thd,khd->thk', query_portion, gate_wide, precision=lax.Precision.HIGHEST))
        gate_values = gate_values.reshape(SBLK, G, group_heads, 3)
        combined = gate_values[..., 0:1] * compressed_out + gate_values[..., 1:2] * selected_out + gate_values[..., 2:3] * window_out
        in_sequence = (token_pos < seq_len[0])[:, None, None, None]
        return jnp.where(in_sequence, combined, 0.0).reshape(SBLK, H, DH).astype(jnp.bfloat16)
    attended = lax.map(one_block, jnp.arange(NQB))
    return attended.reshape(TOKENS, H, DH)
```

```python
import functools
import math

import jax
import jax.numpy as jnp
from jax import lax
from jax.experimental import pallas as pl
from jax.experimental.pallas import tpu as pltpu
from jax.sharding import PartitionSpec as P

H = 64
G = 4
STRIDE = 16
SBLK = 64
NSEL = 16
WIN = 512
PAIR = 2 * SBLK
NEGATIVE = -1e30
MESH = pl.DeviceIdType.MESH
CHUNKS = 4


def share_kernel(count, kv_ref, store_ref, own_sem, send_sem, recv_sem, relay_sem):
    rows = kv_ref.shape[0]
    part = rows // CHUNKS
    me = lax.axis_index("ctx")
    side = lax.rem(me, 2)
    partner = me + 1 - 2 * side
    barrier = pltpu.get_barrier_semaphore()
    for step in range(1, count):
        pl.semaphore_signal(
            barrier, inc=1, device_id={"ctx": lax.rem(me + step, count)}, device_id_type=MESH
        )
    pl.semaphore_wait(barrier, count - 1)

    def piece(owner, chunk):
        return pl.ds(pl.multiple_of(owner * rows + chunk * part, part), part)

    def own_copy(slot, target, chunk):
        return pltpu.make_async_remote_copy(
            src_ref=kv_ref.at[pl.ds(chunk * part, part)],
            dst_ref=store_ref.at[piece(me, chunk)],
            send_sem=send_sem.at[slot, chunk],
            recv_sem=recv_sem.at[me, chunk],
            device_id={"ctx": target},
            device_id_type=MESH,
        )

    def relay_copy(slot, owner, chunk):
        return pltpu.make_async_remote_copy(
            src_ref=store_ref.at[piece(owner, chunk)],
            dst_ref=store_ref.at[piece(owner, chunk)],
            send_sem=relay_sem.at[slot, chunk],
            recv_sem=recv_sem.at[owner, chunk],
            device_id={"ctx": partner},
            device_id_type=MESH,
        )

    hops = range(2, count, 2)
    for chunk in range(CHUNKS):
        for hop in hops:

            @pl.when(me + hop < count)
            def _():
                own_copy(hop // 2, me + hop, chunk).start()

    @pl.when(side == 0)
    def _():
        for chunk in range(CHUNKS):
            own_copy(0, partner, chunk).start()

    mine = pltpu.make_async_copy(
        kv_ref, store_ref.at[pl.ds(pl.multiple_of(me * rows, rows), rows)], own_sem
    )
    mine.start()
    for chunk in range(CHUNKS):
        for hop in hops:

            @pl.when(me >= hop)
            def _():
                relay = relay_copy(hop // 2, me - hop, chunk)
                relay.wait_recv()
                relay.start()

    @pl.when(side == 1)
    def _():
        for chunk in range(CHUNKS):
            relay_copy(0, me - 1, chunk).wait_recv()

    for chunk in range(CHUNKS):
        for hop in hops:

            @pl.when(me >= hop)
            def _():
                relay_copy(hop // 2, me - side - hop + 1 - side, chunk).wait_recv()
                relay_copy(hop // 2, me - hop, chunk).wait_send()

            @pl.when(me + hop < count)
            def _():
                own_copy(hop // 2, me + hop, chunk).wait_send()

    @pl.when(side == 0)
    def _():
        for chunk in range(CHUNKS):
            own_copy(0, partner, chunk).wait_send()

    mine.wait()


def share(kv, count):
    rows, width = kv.shape
    return pl.pallas_call(
        functools.partial(share_kernel, count),
        out_shape=jax.ShapeDtypeStruct((count * rows, width), kv.dtype),
        in_specs=[pl.BlockSpec(memory_space=pltpu.VMEM)],
        out_specs=pl.BlockSpec(memory_space=pltpu.VMEM),
        scratch_shapes=[
            pltpu.SemaphoreType.DMA,
            pltpu.SemaphoreType.DMA((count // 2, CHUNKS)),
            pltpu.SemaphoreType.DMA((count, CHUNKS)),
            pltpu.SemaphoreType.DMA((count // 2, CHUNKS)),
        ],
        compiler_params=pltpu.CompilerParams(collective_id=0, has_side_effects=True),
    )(kv)


def dot_t(a, b):
    return lax.dot_general(a, b, (((1,), (1,)), ((), ())), preferred_element_type=jnp.float32)


def attend_kernel(
    heads, rows, tile,
    choice, meta, q_ref, gate_ref, store_ref, cw_ref, out_ref,
    values_one, lead_sum, own_sum, comp_k, comp_v, sel_k, sel_v, win_k, win_v,
):
    step = pl.program_id(0)
    position = meta[0]
    seq_len = meta[1]
    width = q_ref.shape[1]
    comp_total = comp_k.shape[0]
    factor = math.log2(math.e) / math.sqrt(width)

    @pl.when(step == 0)
    def _():
        live = (position + 1) * rows
        lead_sum[...] = jnp.zeros_like(lead_sum)
        own_sum[...] = jnp.zeros_like(own_sum)
        span = 16 * STRIDE
        first = jnp.concatenate([cw_ref[0, :STRIDE], cw_ref[1, :STRIDE]], axis=1)
        second = jnp.concatenate([cw_ref[0, STRIDE:], cw_ref[1, STRIDE:]], axis=1)

        def summarize(index, _):
            at = pl.ds(pl.multiple_of(index * span, span), span)
            both = store_ref[at, :]
            values_one[at, :width] = both[:, width:]
            values_one[at, width:] = jnp.ones((span, width), jnp.bfloat16)
            wide = both.astype(jnp.float32).reshape(16, STRIDE, 2 * width)
            lead_sum[pl.ds(pl.multiple_of(index * 16 + 8, 8), 16), :] = jnp.sum(
                wide * first[None], axis=1
            )
            own_sum[pl.ds(pl.multiple_of(index * 16, 16), 16), :] = jnp.sum(
                wide * second[None], axis=1
            )
            return 0

        lax.fori_loop(0, live // span, summarize, 0)
        merged = (lead_sum[7 : 7 + comp_total, :] + own_sum[...]).astype(jnp.bfloat16)
        known = lax.broadcasted_iota(jnp.int32, merged.shape, 0) < live // STRIDE
        merged = jnp.where(known, merged, jnp.zeros_like(merged))
        comp_k[...] = merged[:, :width]
        comp_v[:, :width] = merged[:, width:]
        comp_v[:, width:] = jnp.ones((comp_total, width), jnp.bfloat16)

    start = position * rows + step * SBLK

    @pl.when(start >= seq_len)
    def _():
        out_ref[...] = jnp.zeros_like(out_ref)

    @pl.when(start < seq_len)
    def _():
        block = position * (rows // SBLK) + step
        half = lax.rem(step, 2) * SBLK
        base = start - half
        count = jnp.int32(0)
        for k in range(NSEL):
            count = count + (choice[step * NSEL + k] <= block).astype(jnp.int32)
        others = count - 1
        for k in range(NSEL):
            if k == NSEL - 1:
                picked = block
            else:
                picked = choice[step * NSEL + k + (k >= others).astype(jnp.int32)]
            at = pl.ds(pl.multiple_of(picked * SBLK, SBLK), SBLK)
            sel_k[k * SBLK : (k + 1) * SBLK, :] = store_ref[at, :width]
            sel_v[k * SBLK : (k + 1) * SBLK, :] = values_one[at, :]
        full_at = jnp.maximum(base - WIN + PAIR, 0)
        edge_at = jnp.maximum(base - WIN, 0)
        for target, source, length in (
            (0, full_at, WIN - PAIR),
            (WIN - PAIR, base, PAIR),
            (WIN, edge_at, PAIR),
        ):
            at = pl.ds(pl.multiple_of(source, PAIR), length)
            win_k[target : target + length, :] = store_ref[at, :width]
            win_v[target : target + length, :] = values_one[at, :]

        def col_of(n):
            return lax.broadcasted_iota(jnp.int32, (1, n), 1)

        full_bias = jnp.where(col_of(WIN - PAIR) + full_at < base, 0.0, NEGATIVE)
        edge_bias = jnp.where(base >= WIN, 0.0, NEGATIVE)
        early = (NSEL - 2) * SBLK
        sel_bias = jnp.where(col_of(early) < others * SBLK, 0.0, NEGATIVE)
        late_col = col_of(PAIR)
        late_from = jnp.where(
            late_col < SBLK, jnp.where(others >= NSEL - 1, -1, SBLK), late_col - SBLK
        )
        comp_end = col_of(comp_total) * STRIDE + (STRIDE - 1)

        for part in range(SBLK * heads // tile):
            at = slice(part * tile, (part + 1) * tile)
            q = q_ref[at, :]
            row = (
                lax.broadcasted_iota(jnp.int32, (tile, 1), 0) + part * tile
            ) // heads
            token = row + start

            def weigh(scores, vals):
                largest = jnp.max(scores, axis=1, keepdims=True)
                return jnp.exp2((scores - largest) * factor)

            def finish(probs, vals):
                acc = jnp.dot(
                    probs.astype(jnp.bfloat16), vals, preferred_element_type=jnp.float32
                )
                return acc[:, :width] / jnp.maximum(acc[:, width:], 1.0)

            scores = dot_t(q, comp_k[...])
            scores = jnp.where(comp_end <= token, scores, NEGATIVE)
            compressed = finish(weigh(scores, None), comp_v[...])
            compressed = jnp.where(token >= STRIDE - 1, compressed, 0.0)

            scores = dot_t(q, sel_k[...])
            scores = jnp.concatenate(
                [
                    scores[:, :early] + sel_bias,
                    jnp.where(late_from <= row, scores[:, early:], NEGATIVE),
                ],
                axis=1,
            )
            selected = finish(weigh(scores, None), sel_v[...])

            scores = dot_t(q, win_k[...])
            inside = late_col <= row + half
            scores = jnp.concatenate(
                [
                    scores[:, : WIN - PAIR] + full_bias,
                    jnp.where(
                        inside, scores[:, WIN - PAIR : WIN], scores[:, WIN:] + edge_bias
                    ),
                ],
                axis=1,
            )
            probs = weigh(scores, None)
            mixed = probs[:, WIN - PAIR :]
            probs = jnp.concatenate(
                [
                    probs[:, : WIN - PAIR],
                    jnp.where(inside, mixed, 0.0),
                    jnp.where(inside, 0.0, mixed),
                ],
                axis=1,
            )
            window = finish(probs, win_v[...])

            wide = q.astype(jnp.float32)
            gates = [
                jax.nn.sigmoid(
                    jnp.sum(wide * gate_ref[k].astype(jnp.float32), axis=1, keepdims=True)
                )
                for k in range(3)
            ]
            combined = gates[0] * compressed + gates[1] * selected + gates[2] * window
            out_ref[at, :] = jnp.where(token < seq_len, combined, 0.0).astype(jnp.bfloat16)


def attend(queries, gate_weight, store, compress_weight, choice, meta, rows):
    total_rows, width = queries.shape
    heads = gate_weight.shape[1]
    block_rows = SBLK * heads
    tile = min(256, block_rows)
    tokens = store.shape[0]
    comp_total = tokens // STRIDE
    gates = jnp.tile(gate_weight, (1, tile // heads, 1))
    whole = pl.BlockSpec(memory_space=pltpu.VMEM)
    return pl.pallas_call(
        functools.partial(attend_kernel, heads, rows, tile),
        grid_spec=pltpu.PrefetchScalarGridSpec(
            num_scalar_prefetch=2,
            grid=(rows // SBLK,),
            in_specs=[
                pl.BlockSpec((block_rows, width), lambda i, *_: (i, 0)),
                whole,
                whole,
                whole,
            ],
            out_specs=pl.BlockSpec((block_rows, width), lambda i, *_: (i, 0)),
            scratch_shapes=[
                pltpu.VMEM((tokens, 2 * width), jnp.bfloat16),
                pltpu.VMEM((comp_total + 8, 2 * width), jnp.float32),
                pltpu.VMEM((comp_total, 2 * width), jnp.float32),
                pltpu.VMEM((comp_total, width), jnp.bfloat16),
                pltpu.VMEM((comp_total, 2 * width), jnp.bfloat16),
                pltpu.VMEM((NSEL * SBLK, width), jnp.bfloat16),
                pltpu.VMEM((NSEL * SBLK, 2 * width), jnp.bfloat16),
                pltpu.VMEM((WIN + PAIR, width), jnp.bfloat16),
                pltpu.VMEM((WIN + PAIR, 2 * width), jnp.bfloat16),
            ],
        ),
        out_shape=jax.ShapeDtypeStruct((total_rows, width), jnp.bfloat16),
        compiler_params=pltpu.CompilerParams(
            dimension_semantics=("arbitrary",), vmem_limit_bytes=60000 * 1024
        ),
    )(choice, meta, queries, gates, store, compress_weight)


def per_device(queries, keys, values, compress_weight, gate_weight, selection, seq_len):
    rows, heads, width = queries.shape
    count = lax.axis_size("ctx")
    position = lax.axis_index("ctx")
    group = lax.axis_index("head") * heads // (H // G)
    key_mine = lax.dynamic_index_in_dim(keys, group, 1, keepdims=False)
    value_mine = lax.dynamic_index_in_dim(values, group, 1, keepdims=False)
    kv = jnp.concatenate([key_mine, value_mine], axis=1)
    store = share(kv, count)
    per_dev = rows // SBLK
    choice = lax.dynamic_slice(
        selection, (position * per_dev, group, 0), (per_dev, 1, NSEL)
    ).reshape(-1)
    meta = jnp.stack([position.astype(jnp.int32), seq_len[0]])
    out = attend(
        queries.reshape(rows * heads, width),
        gate_weight, store, compress_weight, choice, meta, rows,
    )
    return out.reshape(rows, heads, width)


def solution(mesh):
    return jax.shard_map(
        per_device,
        mesh=mesh,
        in_specs=(
            P(("grp", "ctx"), "head", None),
            P(("grp", "ctx"), None, None),
            P(("grp", "ctx"), None, None),
            P(),
            P(None, "head", None),
            P("grp", None, None),
            P("grp"),
        ),
        out_specs=P(("grp", "ctx"), "head", None),
        check_vma=False,
    )
```

```python
import functools
import math

import jax
import jax.numpy as jnp
from jax import lax
from jax.experimental import pallas as pl
from jax.experimental.pallas import tpu as pltpu
from jax.sharding import PartitionSpec as P

H = 64
G = 4
STRIDE = 16
SBLK = 64
NSEL = 16
WIN = 512
PAIR = 2 * SBLK
NEGATIVE = -1e30
MESH = pl.DeviceIdType.MESH
CHUNKS = 4


def share_kernel(count, kv_ref, store_ref, own_sem, send_sem, recv_sem, relay_sem):
    rows = kv_ref.shape[0]
    part = rows // CHUNKS
    me = lax.axis_index("ctx")
    side = lax.rem(me, 2)
    partner = me + 1 - 2 * side
    barrier = pltpu.get_barrier_semaphore()
    for step in range(1, count):
        pl.semaphore_signal(
            barrier, inc=1, device_id={"ctx": lax.rem(me + step, count)}, device_id_type=MESH
        )
    pl.semaphore_wait(barrier, count - 1)

    def piece(owner, chunk):
        return pl.ds(pl.multiple_of(owner * rows + chunk * part, part), part)

    def own_copy(slot, target, chunk):
        return pltpu.make_async_remote_copy(
            src_ref=kv_ref.at[pl.ds(chunk * part, part)],
            dst_ref=store_ref.at[piece(me, chunk)],
            send_sem=send_sem.at[slot, chunk],
            recv_sem=recv_sem.at[me, chunk],
            device_id={"ctx": target},
            device_id_type=MESH,
        )

    def relay_copy(slot, owner, chunk):
        return pltpu.make_async_remote_copy(
            src_ref=store_ref.at[piece(owner, chunk)],
            dst_ref=store_ref.at[piece(owner, chunk)],
            send_sem=relay_sem.at[slot, chunk],
            recv_sem=recv_sem.at[owner, chunk],
            device_id={"ctx": partner},
            device_id_type=MESH,
        )

    hops = range(2, count, 2)
    for chunk in range(CHUNKS):
        for hop in hops:

            @pl.when(me + hop < count)
            def _():
                own_copy(hop // 2, me + hop, chunk).start()

    @pl.when(side == 0)
    def _():
        for chunk in range(CHUNKS):
            own_copy(0, partner, chunk).start()

    mine = pltpu.make_async_copy(
        kv_ref, store_ref.at[pl.ds(pl.multiple_of(me * rows, rows), rows)], own_sem
    )
    mine.start()
    for chunk in range(CHUNKS):
        for hop in hops:

            @pl.when(me >= hop)
            def _():
                relay = relay_copy(hop // 2, me - hop, chunk)
                relay.wait_recv()
                relay.start()

    @pl.when(side == 1)
    def _():
        for chunk in range(CHUNKS):
            relay_copy(0, me - 1, chunk).wait_recv()

    for chunk in range(CHUNKS):
        for hop in hops:

            @pl.when(me >= hop)
            def _():
                relay_copy(hop // 2, me - side - hop + 1 - side, chunk).wait_recv()
                relay_copy(hop // 2, me - hop, chunk).wait_send()

            @pl.when(me + hop < count)
            def _():
                own_copy(hop // 2, me + hop, chunk).wait_send()

    @pl.when(side == 0)
    def _():
        for chunk in range(CHUNKS):
            own_copy(0, partner, chunk).wait_send()

    mine.wait()


def share(kv, count):
    rows, width = kv.shape
    return pl.pallas_call(
        functools.partial(share_kernel, count),
        out_shape=jax.ShapeDtypeStruct((count * rows, width), kv.dtype),
        in_specs=[pl.BlockSpec(memory_space=pltpu.VMEM)],
        out_specs=pl.BlockSpec(memory_space=pltpu.VMEM),
        scratch_shapes=[
            pltpu.SemaphoreType.DMA,
            pltpu.SemaphoreType.DMA((count // 2, CHUNKS)),
            pltpu.SemaphoreType.DMA((count, CHUNKS)),
            pltpu.SemaphoreType.DMA((count // 2, CHUNKS)),
        ],
        compiler_params=pltpu.CompilerParams(collective_id=0, has_side_effects=True),
    )(kv)


def dot_t(a, b):
    return lax.dot_general(a, b, (((1,), (1,)), ((), ())), preferred_element_type=jnp.float32)


def dot_both(a, b):
    return dot_t(a, jnp.concatenate([b, b], axis=1))


def attend_kernel(
    heads, rows, tile,
    choice, meta, q_ref, gate_ref, store_ref, cw_ref, out_ref,
    values_one, lead_sum, own_sum, comp_k, comp_v, sel_k, sel_v, win_k, win_v,
):
    step = pl.program_id(0)
    position = meta[0]
    seq_len = meta[1]
    width = q_ref.shape[1]
    comp_total = comp_k.shape[0]
    factor = math.log2(math.e) / math.sqrt(width)

    @pl.when(step == 0)
    def _():
        live = (position + 1) * rows
        lead_sum[...] = jnp.zeros_like(lead_sum)
        own_sum[...] = jnp.zeros_like(own_sum)
        span = 16 * STRIDE
        first = jnp.concatenate([cw_ref[0, :STRIDE], cw_ref[1, :STRIDE]], axis=1)
        second = jnp.concatenate([cw_ref[0, STRIDE:], cw_ref[1, STRIDE:]], axis=1)

        def summarize(index, _):
            at = pl.ds(pl.multiple_of(index * span, span), span)
            both = store_ref[at, :]
            values_one[at, :width] = both[:, width:]
            values_one[at, width:] = jnp.ones((span, width), jnp.bfloat16)
            wide = both.astype(jnp.float32).reshape(16, STRIDE, 2 * width)
            lead_sum[pl.ds(pl.multiple_of(index * 16 + 8, 8), 16), :] = jnp.sum(
                wide * first[None], axis=1
            )
            own_sum[pl.ds(pl.multiple_of(index * 16, 16), 16), :] = jnp.sum(
                wide * second[None], axis=1
            )
            return 0

        lax.fori_loop(0, live // span, summarize, 0)
        merged = (lead_sum[7 : 7 + comp_total, :] + own_sum[...]).astype(jnp.bfloat16)
        known = lax.broadcasted_iota(jnp.int32, merged.shape, 0) < live // STRIDE
        merged = jnp.where(known, merged, jnp.zeros_like(merged))
        comp_k[...] = merged[:, :width]
        comp_v[:, :width] = merged[:, width:]
        comp_v[:, width:] = jnp.ones((comp_total, width), jnp.bfloat16)

    start = position * rows + step * SBLK

    @pl.when(start >= seq_len)
    def _():
        out_ref[...] = jnp.zeros_like(out_ref)

    @pl.when(start < seq_len)
    def _():
        block = position * (rows // SBLK) + step
        half = lax.rem(step, 2) * SBLK
        base = start - half
        count = jnp.int32(0)
        for k in range(NSEL):
            count = count + (choice[step * NSEL + k] <= block).astype(jnp.int32)
        others = count - 1
        anchor = store_ref[pl.ds(pl.multiple_of(start, SBLK), 16), :width][:1]

        def place(k_out, v_out, target, source, length, valid):
            at = pl.ds(pl.multiple_of(source, SBLK), length)
            rows_at = slice(target, target + length)
            held = values_one[at, :]
            k_out[rows_at, :] = jnp.where(valid, store_ref[at, :width], anchor)
            v_out[rows_at, :] = jnp.where(valid, held, jnp.zeros_like(held))

        for k in range(NSEL):
            if k == NSEL - 1:
                picked = block
            else:
                picked = choice[step * NSEL + k + (k >= others).astype(jnp.int32)]
            valid = (k < others) | (k == NSEL - 1)
            place(sel_k, sel_v, k * SBLK, picked * SBLK, SBLK, valid)
        for k in range(WIN // PAIR):
            source = base - (WIN - PAIR) + k * PAIR
            place(win_k, win_v, k * PAIR, jnp.maximum(source, 0), PAIR, source >= 0)
        place(win_k, win_v, WIN, jnp.maximum(base - WIN, 0), PAIR, base >= WIN)

        def col_of(n):
            return lax.broadcasted_iota(jnp.int32, (1, n), 1)

        early = (NSEL - 2) * SBLK
        late_col = col_of(PAIR)
        late_from = jnp.where(late_col < SBLK, -1, late_col - SBLK)
        comp_end = col_of(comp_total) * STRIDE + (STRIDE - 1)

        for part in range(SBLK * heads // tile):
            at = slice(part * tile, (part + 1) * tile)
            q = q_ref[at, :]
            scaled = q.astype(jnp.float32) * factor
            upper = scaled.astype(jnp.bfloat16)
            lower = (scaled - upper.astype(jnp.float32)).astype(jnp.bfloat16)
            q_both = jnp.concatenate([upper, lower], axis=1)
            row = (
                lax.broadcasted_iota(jnp.int32, (tile, 1), 0) + part * tile
            ) // heads
            token = row + start

            def weigh(scores):
                largest = jnp.max(scores, axis=1, keepdims=True)
                return jnp.exp2(scores - largest)

            def finish(probs, vals):
                acc = jnp.dot(
                    probs.astype(jnp.bfloat16), vals, preferred_element_type=jnp.float32
                )
                return acc[:, :width] / jnp.maximum(acc[:, width:], 1.0)

            scores = dot_both(q_both, comp_k[...])
            scores = jnp.where(comp_end <= token, scores, NEGATIVE)
            compressed = finish(weigh(scores), comp_v[...])
            compressed = jnp.where(token >= STRIDE - 1, compressed, 0.0)

            scores = dot_both(q_both, sel_k[...])
            scores = jnp.concatenate(
                [
                    scores[:, :early],
                    jnp.where(late_from <= row, scores[:, early:], NEGATIVE),
                ],
                axis=1,
            )
            selected = finish(weigh(scores), sel_v[...])

            scores = dot_both(q_both, win_k[...])
            inside = late_col <= row + half
            scores = jnp.concatenate(
                [
                    scores[:, : WIN - PAIR],
                    jnp.where(
                        inside, scores[:, WIN - PAIR : WIN], scores[:, WIN:]
                    ),
                ],
                axis=1,
            )
            probs = weigh(scores)
            mixed = probs[:, WIN - PAIR :]
            probs = jnp.concatenate(
                [
                    probs[:, : WIN - PAIR],
                    jnp.where(inside, mixed, 0.0),
                    jnp.where(inside, 0.0, mixed),
                ],
                axis=1,
            )
            window = finish(probs, win_v[...])

            wide = q.astype(jnp.float32).reshape(tile // heads, heads, width)
            gates = [
                jax.nn.sigmoid(
                    jnp.sum(
                        (wide * gate_ref[k].astype(jnp.float32)[None]).reshape(tile, width),
                        axis=1,
                        keepdims=True,
                    )
                )
                for k in range(3)
            ]
            combined = gates[0] * compressed + gates[1] * selected + gates[2] * window
            out_ref[at, :] = jnp.where(token < seq_len, combined, 0.0).astype(jnp.bfloat16)


def attend(queries, gate_weight, store, compress_weight, choice, meta, rows):
    total_rows, width = queries.shape
    heads = gate_weight.shape[1]
    block_rows = SBLK * heads
    tile = min(1024, block_rows)
    tokens = store.shape[0]
    comp_total = tokens // STRIDE
    whole = pl.BlockSpec(memory_space=pltpu.VMEM)
    return pl.pallas_call(
        functools.partial(attend_kernel, heads, rows, tile),
        grid_spec=pltpu.PrefetchScalarGridSpec(
            num_scalar_prefetch=2,
            grid=(rows // SBLK,),
            in_specs=[
                pl.BlockSpec((block_rows, width), lambda i, *_: (i, 0)),
                whole,
                whole,
                whole,
            ],
            out_specs=pl.BlockSpec((block_rows, width), lambda i, *_: (i, 0)),
            scratch_shapes=[
                pltpu.VMEM((tokens, 2 * width), jnp.bfloat16),
                pltpu.VMEM((comp_total + 8, 2 * width), jnp.float32),
                pltpu.VMEM((comp_total, 2 * width), jnp.float32),
                pltpu.VMEM((comp_total, width), jnp.bfloat16),
                pltpu.VMEM((comp_total, 2 * width), jnp.bfloat16),
                pltpu.VMEM((NSEL * SBLK, width), jnp.bfloat16),
                pltpu.VMEM((NSEL * SBLK, 2 * width), jnp.bfloat16),
                pltpu.VMEM((WIN + PAIR, width), jnp.bfloat16),
                pltpu.VMEM((WIN + PAIR, 2 * width), jnp.bfloat16),
            ],
        ),
        out_shape=jax.ShapeDtypeStruct((total_rows, width), jnp.bfloat16),
        compiler_params=pltpu.CompilerParams(
            dimension_semantics=("arbitrary",), vmem_limit_bytes=60000 * 1024
        ),
    )(choice, meta, queries, gate_weight, store, compress_weight)


def per_device(queries, keys, values, compress_weight, gate_weight, selection, seq_len):
    rows, heads, width = queries.shape
    count = lax.axis_size("ctx")
    position = lax.axis_index("ctx")
    group = lax.axis_index("head") * heads // (H // G)
    key_mine = lax.dynamic_index_in_dim(keys, group, 1, keepdims=False)
    value_mine = lax.dynamic_index_in_dim(values, group, 1, keepdims=False)
    kv = jnp.concatenate([key_mine, value_mine], axis=1)
    store = share(kv, count)
    per_dev = rows // SBLK
    choice = lax.dynamic_slice(
        selection, (position * per_dev, group, 0), (per_dev, 1, NSEL)
    ).reshape(-1)
    meta = jnp.stack([position.astype(jnp.int32), seq_len[0]])
    out = attend(
        queries.reshape(rows * heads, width),
        gate_weight, store, compress_weight, choice, meta, rows,
    )
    return out.reshape(rows, heads, width)


def solution(mesh):
    return jax.shard_map(
        per_device,
        mesh=mesh,
        in_specs=(
            P(("grp", "ctx"), "head", None),
            P(("grp", "ctx"), None, None),
            P(("grp", "ctx"), None, None),
            P(),
            P(None, "head", None),
            P("grp", None, None),
            P("grp"),
        ),
        out_specs=P(("grp", "ctx"), "head", None),
        check_vma=False,
    )
```

```python
import functools
import math

import jax
import jax.numpy as jnp
from jax import lax
from jax.experimental import pallas as pl
from jax.experimental.pallas import tpu as pltpu
from jax.sharding import PartitionSpec as P

H = 64
G = 4
STRIDE = 16
SBLK = 64
NSEL = 16
WIN = 512
PAIR = 2 * SBLK
NEGATIVE = -1e30
MESH = pl.DeviceIdType.MESH
CHUNKS = 4


def dot_t(a, b):
    return lax.dot_general(a, b, (((1,), (1,)), ((), ())), preferred_element_type=jnp.float32)


def dot_both(a, b):
    return dot_t(a, jnp.concatenate([b, b], axis=1))


def split_scaled(q):
    scaled = q.astype(jnp.float32) * (math.log2(math.e) / math.sqrt(q.shape[1]))
    upper = scaled.astype(jnp.bfloat16)
    lower = (scaled - upper.astype(jnp.float32)).astype(jnp.bfloat16)
    return jnp.concatenate([upper, lower], axis=1)


def weigh(scores):
    return jnp.exp2(scores - jnp.max(scores, axis=1, keepdims=True))


def finish(probs, vals):
    width = vals.shape[1] // 2
    acc = jnp.dot(probs.astype(jnp.bfloat16), vals, preferred_element_type=jnp.float32)
    return acc[:, :width] / jnp.maximum(acc[:, width:], 1.0)


def window_of(q_both, keys, vals, inside):
    scores = dot_both(q_both, keys)
    scores = jnp.concatenate(
        [
            scores[:, : WIN - PAIR],
            jnp.where(inside, scores[:, WIN - PAIR : WIN], scores[:, WIN:]),
        ],
        axis=1,
    )
    probs = weigh(scores)
    mixed = probs[:, WIN - PAIR :]
    probs = jnp.concatenate(
        [probs[:, : WIN - PAIR], jnp.where(inside, mixed, 0.0), jnp.where(inside, 0.0, mixed)],
        axis=1,
    )
    return finish(probs, vals)


def share_kernel(
    count, heads, kv_ref, q_hbm, store_ref, win_ref,
    q_ref, own_sem, q_sem, send_sem, recv_sem, relay_sem,
):
    rows = kv_ref.shape[0]
    width = kv_ref.shape[1] // 2
    load_q = pltpu.make_async_copy(
        q_hbm.at[pl.ds(WIN * heads, (rows - WIN) * heads)], q_ref, q_sem
    )
    load_q.start()
    part = rows // CHUNKS
    me = lax.axis_index("ctx")
    side = lax.rem(me, 2)
    partner = me + 1 - 2 * side
    barrier = pltpu.get_barrier_semaphore()
    for step in range(1, count):
        pl.semaphore_signal(
            barrier, inc=1, device_id={"ctx": lax.rem(me + step, count)}, device_id_type=MESH
        )
    pl.semaphore_wait(barrier, count - 1)

    def piece(owner, chunk):
        return pl.ds(pl.multiple_of(owner * rows + chunk * part, part), part)

    def own_copy(slot, target, chunk):
        return pltpu.make_async_remote_copy(
            src_ref=kv_ref.at[pl.ds(chunk * part, part)],
            dst_ref=store_ref.at[piece(me, chunk)],
            send_sem=send_sem.at[slot, chunk],
            recv_sem=recv_sem.at[me, chunk],
            device_id={"ctx": target},
            device_id_type=MESH,
        )

    def relay_copy(slot, owner, chunk):
        return pltpu.make_async_remote_copy(
            src_ref=store_ref.at[piece(owner, chunk)],
            dst_ref=store_ref.at[piece(owner, chunk)],
            send_sem=relay_sem.at[slot, chunk],
            recv_sem=recv_sem.at[owner, chunk],
            device_id={"ctx": partner},
            device_id_type=MESH,
        )

    hops = range(2, count, 2)
    for chunk in range(CHUNKS):
        for hop in hops:

            @pl.when(me + hop < count)
            def _():
                own_copy(hop // 2, me + hop, chunk).start()

    @pl.when(side == 0)
    def _():
        for chunk in range(CHUNKS):
            own_copy(0, partner, chunk).start()

    mine = pltpu.make_async_copy(
        kv_ref, store_ref.at[pl.ds(pl.multiple_of(me * rows, rows), rows)], own_sem
    )
    mine.start()
    load_q.wait()
    block_rows = SBLK * heads
    row = lax.broadcasted_iota(jnp.int32, (block_rows, 1), 0) // heads
    late_col = lax.broadcasted_iota(jnp.int32, (1, PAIR), 1)

    def local_window(index, _):
        at = pl.ds(pl.multiple_of(index * block_rows, block_rows), block_rows)
        first = pl.multiple_of((index // 2) * PAIR, PAIR)
        middle = kv_ref[pl.ds(first + PAIR, WIN), :]
        edge = kv_ref[pl.ds(first, PAIR), :]
        near = jnp.concatenate([middle, edge], axis=0)
        vals = jnp.concatenate(
            [near[:, width:], jnp.ones((WIN + PAIR, width), jnp.bfloat16)], axis=1
        )
        inside = late_col <= row + (index % 2) * SBLK
        win_ref[at, :] = window_of(
            split_scaled(q_ref[at, :]), near[:, :width], vals, inside
        ).astype(jnp.bfloat16)
        return 0

    local_steps = (rows - WIN) // SBLK
    per = local_steps // CHUNKS

    def stage(chunk, _):
        lax.fori_loop(
            per * chunk - chunk // CHUNKS,
            per * (chunk + 1)
            - (chunk + 1) // CHUNKS
            - (chunk + 1) // (CHUNKS + 1) * (per - 1),
            local_window,
            0,
        )
        for hop in hops:

            @pl.when((me >= hop) & (chunk < CHUNKS))
            def _():
                relay = relay_copy(hop // 2, me - hop, chunk)
                relay.wait_recv()
                relay.start()

        return 0

    lax.fori_loop(0, CHUNKS + 1, stage, 0)

    @pl.when(side == 1)
    def _():
        for chunk in range(CHUNKS):
            relay_copy(0, me - 1, chunk).wait_recv()

    for chunk in range(CHUNKS):
        for hop in hops:

            @pl.when(me >= hop)
            def _():
                relay_copy(hop // 2, me - side - hop + 1 - side, chunk).wait_recv()
                relay_copy(hop // 2, me - hop, chunk).wait_send()

            @pl.when(me + hop < count)
            def _():
                own_copy(hop // 2, me + hop, chunk).wait_send()

    @pl.when(side == 0)
    def _():
        for chunk in range(CHUNKS):
            own_copy(0, partner, chunk).wait_send()

    mine.wait()


def share(kv, queries, count, heads):
    rows, width = kv.shape
    local_rows = (rows - WIN) * heads
    return pl.pallas_call(
        functools.partial(share_kernel, count, heads),
        out_shape=(
            jax.ShapeDtypeStruct((count * rows, width), kv.dtype),
            jax.ShapeDtypeStruct((local_rows, width // 2), jnp.bfloat16),
        ),
        in_specs=[
            pl.BlockSpec(memory_space=pltpu.VMEM),
            pl.BlockSpec(memory_space=pl.ANY),
        ],
        out_specs=(
            pl.BlockSpec(memory_space=pltpu.VMEM),
            pl.BlockSpec(memory_space=pltpu.VMEM),
        ),
        scratch_shapes=[
            pltpu.VMEM((local_rows, width // 2), jnp.bfloat16),
            pltpu.SemaphoreType.DMA,
            pltpu.SemaphoreType.DMA,
            pltpu.SemaphoreType.DMA((count // 2, CHUNKS)),
            pltpu.SemaphoreType.DMA((count, CHUNKS)),
            pltpu.SemaphoreType.DMA((count // 2, CHUNKS)),
        ],
        compiler_params=pltpu.CompilerParams(
            collective_id=0, has_side_effects=True, vmem_limit_bytes=60000 * 1024
        ),
    )(kv, queries)


def attend_kernel(
    heads, rows, tile,
    choice, meta, q_ref, gate_ref, store_ref, cw_ref, local_ref, out_ref,
    values_one, lead_sum, own_sum, comp_k, comp_v, sel_k, sel_v, win_k, win_v,
):
    step = pl.program_id(0)
    position = meta[0]
    seq_len = meta[1]
    width = q_ref.shape[1]
    comp_total = comp_k.shape[0]

    @pl.when(step == 0)
    def _():
        live = (position + 1) * rows
        lead_sum[...] = jnp.zeros_like(lead_sum)
        own_sum[...] = jnp.zeros_like(own_sum)
        span = 16 * STRIDE
        first = jnp.concatenate([cw_ref[0, :STRIDE], cw_ref[1, :STRIDE]], axis=1)
        second = jnp.concatenate([cw_ref[0, STRIDE:], cw_ref[1, STRIDE:]], axis=1)

        def summarize(index, _):
            at = pl.ds(pl.multiple_of(index * span, span), span)
            both = store_ref[at, :]
            values_one[at, :width] = both[:, width:]
            values_one[at, width:] = jnp.ones((span, width), jnp.bfloat16)
            wide = both.astype(jnp.float32).reshape(16, STRIDE, 2 * width)
            lead_sum[pl.ds(pl.multiple_of(index * 16 + 8, 8), 16), :] = jnp.sum(
                wide * first[None], axis=1
            )
            own_sum[pl.ds(pl.multiple_of(index * 16, 16), 16), :] = jnp.sum(
                wide * second[None], axis=1
            )
            return 0

        lax.fori_loop(0, live // span, summarize, 0)
        merged = (lead_sum[7 : 7 + comp_total, :] + own_sum[...]).astype(jnp.bfloat16)
        known = lax.broadcasted_iota(jnp.int32, merged.shape, 0) < live // STRIDE
        merged = jnp.where(known, merged, jnp.zeros_like(merged))
        comp_k[...] = merged[:, :width]
        comp_v[:, :width] = merged[:, width:]
        comp_v[:, width:] = jnp.ones((comp_total, width), jnp.bfloat16)

    start = position * rows + step * SBLK

    @pl.when(start >= seq_len)
    def _():
        out_ref[...] = jnp.zeros_like(out_ref)

    def run(local):
        block = position * (rows // SBLK) + step
        half = lax.rem(step, 2) * SBLK
        base = start - half
        count = jnp.int32(0)
        for k in range(NSEL):
            count = count + (choice[step * NSEL + k] <= block).astype(jnp.int32)
        others = count - 1
        anchor = store_ref[pl.ds(pl.multiple_of(start, SBLK), 16), :width][:1]

        def place(k_out, v_out, target, source, length, valid):
            at = pl.ds(pl.multiple_of(source, SBLK), length)
            rows_at = slice(target, target + length)
            held = values_one[at, :]
            k_out[rows_at, :] = jnp.where(valid, store_ref[at, :width], anchor)
            v_out[rows_at, :] = jnp.where(valid, held, jnp.zeros_like(held))

        for k in range(NSEL):
            if k == NSEL - 1:
                picked = block
            else:
                picked = choice[step * NSEL + k + (k >= others).astype(jnp.int32)]
            valid = (k < others) | (k == NSEL - 1)
            place(sel_k, sel_v, k * SBLK, picked * SBLK, SBLK, valid)
        for k in range(0 if local else WIN // PAIR):
            source = base - (WIN - PAIR) + k * PAIR
            place(win_k, win_v, k * PAIR, jnp.maximum(source, 0), PAIR, source >= 0)
        if not local:
            place(win_k, win_v, WIN, jnp.maximum(base - WIN, 0), PAIR, base >= WIN)

        def col_of(n):
            return lax.broadcasted_iota(jnp.int32, (1, n), 1)

        early = (NSEL - 2) * SBLK
        late_col = col_of(PAIR)
        late_from = jnp.where(late_col < SBLK, -1, late_col - SBLK)
        comp_end = col_of(comp_total) * STRIDE + (STRIDE - 1)

        for part in range(SBLK * heads // tile):
            at = slice(part * tile, (part + 1) * tile)
            q = q_ref[at, :]
            q_both = split_scaled(q)
            row = (
                lax.broadcasted_iota(jnp.int32, (tile, 1), 0) + part * tile
            ) // heads
            token = row + start

            scores = dot_both(q_both, comp_k[...])
            scores = jnp.where(comp_end <= token, scores, NEGATIVE)
            compressed = finish(weigh(scores), comp_v[...])
            compressed = jnp.where(token >= STRIDE - 1, compressed, 0.0)

            scores = dot_both(q_both, sel_k[...])
            scores = jnp.concatenate(
                [
                    scores[:, :early],
                    jnp.where(late_from <= row, scores[:, early:], NEGATIVE),
                ],
                axis=1,
            )
            selected = finish(weigh(scores), sel_v[...])

            if local:
                window = local_ref[at, :].astype(jnp.float32)
            else:
                window = window_of(q_both, win_k[...], win_v[...], late_col <= row + half)

            wide = q.astype(jnp.float32).reshape(tile // heads, heads, width)
            gates = [
                jax.nn.sigmoid(
                    jnp.sum(
                        (wide * gate_ref[k].astype(jnp.float32)[None]).reshape(tile, width),
                        axis=1,
                        keepdims=True,
                    )
                )
                for k in range(3)
            ]
            combined = gates[0] * compressed + gates[1] * selected + gates[2] * window
            out_ref[at, :] = jnp.where(token < seq_len, combined, 0.0).astype(jnp.bfloat16)

    far = WIN // SBLK

    @pl.when((start < seq_len) & (step < far))
    def _():
        run(False)

    @pl.when((start < seq_len) & (step >= far))
    def _():
        run(True)


def attend(queries, gate_weight, store, compress_weight, choice, meta, local, rows):
    total_rows, width = queries.shape
    heads = gate_weight.shape[1]
    block_rows = SBLK * heads
    tile = min(1024, block_rows)
    tokens = store.shape[0]
    comp_total = tokens // STRIDE
    whole = pl.BlockSpec(memory_space=pltpu.VMEM)
    return pl.pallas_call(
        functools.partial(attend_kernel, heads, rows, tile),
        grid_spec=pltpu.PrefetchScalarGridSpec(
            num_scalar_prefetch=2,
            grid=(rows // SBLK,),
            in_specs=[
                pl.BlockSpec((block_rows, width), lambda i, *_: (i, 0)),
                whole,
                whole,
                whole,
                pl.BlockSpec(
                    (block_rows, width),
                    lambda i, *_: (jnp.maximum(i - WIN // SBLK, 0), 0),
                ),
            ],
            out_specs=pl.BlockSpec((block_rows, width), lambda i, *_: (i, 0)),
            scratch_shapes=[
                pltpu.VMEM((tokens, 2 * width), jnp.bfloat16),
                pltpu.VMEM((comp_total + 8, 2 * width), jnp.float32),
                pltpu.VMEM((comp_total, 2 * width), jnp.float32),
                pltpu.VMEM((comp_total, width), jnp.bfloat16),
                pltpu.VMEM((comp_total, 2 * width), jnp.bfloat16),
                pltpu.VMEM((NSEL * SBLK, width), jnp.bfloat16),
                pltpu.VMEM((NSEL * SBLK, 2 * width), jnp.bfloat16),
                pltpu.VMEM((WIN + PAIR, width), jnp.bfloat16),
                pltpu.VMEM((WIN + PAIR, 2 * width), jnp.bfloat16),
            ],
        ),
        out_shape=jax.ShapeDtypeStruct((total_rows, width), jnp.bfloat16),
        compiler_params=pltpu.CompilerParams(
            dimension_semantics=("arbitrary",), vmem_limit_bytes=60000 * 1024
        ),
    )(choice, meta, queries, gate_weight, store, compress_weight, local)


def per_device(queries, keys, values, compress_weight, gate_weight, selection, seq_len):
    rows, heads, width = queries.shape
    count = lax.axis_size("ctx")
    position = lax.axis_index("ctx")
    group = lax.axis_index("head") * heads // (H // G)
    key_mine = lax.dynamic_index_in_dim(keys, group, 1, keepdims=False)
    value_mine = lax.dynamic_index_in_dim(values, group, 1, keepdims=False)
    kv = jnp.concatenate([key_mine, value_mine], axis=1)
    flat = queries.reshape(rows * heads, width)
    store, local = share(kv, flat, count, heads)
    per_dev = rows // SBLK
    choice = lax.dynamic_slice(
        selection, (position * per_dev, group, 0), (per_dev, 1, NSEL)
    ).reshape(-1)
    meta = jnp.stack([position.astype(jnp.int32), seq_len[0]])
    out = attend(
        flat, gate_weight, store, compress_weight, choice, meta, local, rows,
    )
    return out.reshape(rows, heads, width)


def solution(mesh):
    return jax.shard_map(
        per_device,
        mesh=mesh,
        in_specs=(
            P(("grp", "ctx"), "head", None),
            P(("grp", "ctx"), None, None),
            P(("grp", "ctx"), None, None),
            P(),
            P(None, "head", None),
            P("grp", None, None),
            P("grp"),
        ),
        out_specs=P(("grp", "ctx"), "head", None),
        check_vma=False,
    )
```

```python
import functools
import math

import jax
import jax.numpy as jnp
from jax import lax
from jax.experimental import pallas as pl
from jax.experimental.pallas import tpu as pltpu
from jax.sharding import PartitionSpec as P

H = 64
G = 4
STRIDE = 16
SBLK = 64
NSEL = 16
WIN = 512
PAIR = 2 * SBLK
NEGATIVE = -1e30
MESH = pl.DeviceIdType.MESH
CHUNKS = 4


def dot_t(a, b):
    return lax.dot_general(a, b, (((1,), (1,)), ((), ())), preferred_element_type=jnp.float32)


def dot_both(a, b):
    return dot_t(a, jnp.concatenate([b, b], axis=1))


def split_scaled(q):
    scaled = q.astype(jnp.float32) * (math.log2(math.e) / math.sqrt(q.shape[1]))
    upper = scaled.astype(jnp.bfloat16)
    lower = (scaled - upper.astype(jnp.float32)).astype(jnp.bfloat16)
    return jnp.concatenate([upper, lower], axis=1)


def weigh(scores):
    return jnp.exp2(scores - jnp.max(scores, axis=1, keepdims=True))


def finish(probs, vals):
    width = vals.shape[1] // 2
    acc = jnp.dot(probs.astype(jnp.bfloat16), vals, preferred_element_type=jnp.float32)
    return acc[:, :width] / jnp.maximum(acc[:, width:], 1.0)


def window_of(q_both, keys, vals, inside):
    scores = dot_both(q_both, keys)
    scores = jnp.concatenate(
        [
            scores[:, : WIN - PAIR],
            jnp.where(inside, scores[:, WIN - PAIR : WIN], scores[:, WIN:]),
        ],
        axis=1,
    )
    probs = weigh(scores)
    mixed = probs[:, WIN - PAIR :]
    probs = jnp.concatenate(
        [probs[:, : WIN - PAIR], jnp.where(inside, mixed, 0.0), jnp.where(inside, 0.0, mixed)],
        axis=1,
    )
    return finish(probs, vals)


def share_kernel(
    count, heads, kv_ref, q_hbm, store_ref, win_ref,
    q_ref, own_sem, q_sem, send_sem, recv_sem, relay_sem,
):
    rows = kv_ref.shape[0]
    width = kv_ref.shape[1] // 2
    load_q = pltpu.make_async_copy(
        q_hbm.at[pl.ds(WIN * heads, (rows - WIN) * heads)], q_ref, q_sem
    )
    load_q.start()
    part = rows // CHUNKS
    me = lax.axis_index("ctx")
    side = lax.rem(me, 2)
    partner = me + 1 - 2 * side
    barrier = pltpu.get_barrier_semaphore()
    for step in range(1, count):
        pl.semaphore_signal(
            barrier, inc=1, device_id={"ctx": lax.rem(me + step, count)}, device_id_type=MESH
        )
    pl.semaphore_wait(barrier, count - 1)

    def piece(owner, chunk):
        return pl.ds(pl.multiple_of(owner * rows + chunk * part, part), part)

    def own_copy(slot, target, chunk):
        return pltpu.make_async_remote_copy(
            src_ref=kv_ref.at[pl.ds(chunk * part, part)],
            dst_ref=store_ref.at[piece(me, chunk)],
            send_sem=send_sem.at[slot, chunk],
            recv_sem=recv_sem.at[me, chunk],
            device_id={"ctx": target},
            device_id_type=MESH,
        )

    def relay_copy(slot, owner, chunk):
        return pltpu.make_async_remote_copy(
            src_ref=store_ref.at[piece(owner, chunk)],
            dst_ref=store_ref.at[piece(owner, chunk)],
            send_sem=relay_sem.at[slot, chunk],
            recv_sem=recv_sem.at[owner, chunk],
            device_id={"ctx": partner},
            device_id_type=MESH,
        )

    hops = range(2, count, 2)
    for chunk in range(CHUNKS):
        for hop in hops:

            @pl.when(me + hop < count)
            def _():
                own_copy(hop // 2, me + hop, chunk).start()

    @pl.when(side == 0)
    def _():
        for chunk in range(CHUNKS):
            own_copy(0, partner, chunk).start()

    mine = pltpu.make_async_copy(
        kv_ref, store_ref.at[pl.ds(pl.multiple_of(me * rows, rows), rows)], own_sem
    )
    mine.start()
    load_q.wait()
    block_rows = PAIR * heads
    row = lax.broadcasted_iota(jnp.int32, (block_rows, 1), 0) // heads
    late_col = lax.broadcasted_iota(jnp.int32, (1, PAIR), 1)

    def local_window(index, _):
        at = pl.ds(pl.multiple_of(index * block_rows, block_rows), block_rows)
        first = pl.multiple_of(index * PAIR, PAIR)
        middle = kv_ref[pl.ds(first + PAIR, WIN), :]
        edge = kv_ref[pl.ds(first, PAIR), :]
        near = jnp.concatenate([middle, edge], axis=0)
        vals = jnp.concatenate(
            [near[:, width:], jnp.ones((WIN + PAIR, width), jnp.bfloat16)], axis=1
        )
        inside = late_col <= row
        win_ref[at, :] = window_of(
            split_scaled(q_ref[at, :]), near[:, :width], vals, inside
        ).astype(jnp.bfloat16)
        return 0

    local_steps = (rows - WIN) // PAIR
    per = local_steps // CHUNKS

    def stage(chunk, _):
        lax.fori_loop(
            per * chunk - chunk // CHUNKS,
            per * (chunk + 1)
            - (chunk + 1) // CHUNKS
            - (chunk + 1) // (CHUNKS + 1) * (per - 1),
            local_window,
            0,
        )
        for hop in hops:

            @pl.when((me >= hop) & (chunk < CHUNKS))
            def _():
                relay = relay_copy(hop // 2, me - hop, chunk)
                relay.wait_recv()
                relay.start()

        return 0

    lax.fori_loop(0, CHUNKS + 1, stage, 0)

    @pl.when(side == 1)
    def _():
        for chunk in range(CHUNKS):
            relay_copy(0, me - 1, chunk).wait_recv()

    for chunk in range(CHUNKS):
        for hop in hops:

            @pl.when(me >= hop)
            def _():
                relay_copy(hop // 2, me - side - hop + 1 - side, chunk).wait_recv()
                relay_copy(hop // 2, me - hop, chunk).wait_send()

            @pl.when(me + hop < count)
            def _():
                own_copy(hop // 2, me + hop, chunk).wait_send()

    @pl.when(side == 0)
    def _():
        for chunk in range(CHUNKS):
            own_copy(0, partner, chunk).wait_send()

    mine.wait()


def share(kv, queries, count, heads):
    rows, width = kv.shape
    local_rows = (rows - WIN) * heads
    return pl.pallas_call(
        functools.partial(share_kernel, count, heads),
        out_shape=(
            jax.ShapeDtypeStruct((count * rows, width), kv.dtype),
            jax.ShapeDtypeStruct((local_rows, width // 2), jnp.bfloat16),
        ),
        in_specs=[
            pl.BlockSpec(memory_space=pltpu.VMEM),
            pl.BlockSpec(memory_space=pl.ANY),
        ],
        out_specs=(
            pl.BlockSpec(memory_space=pltpu.VMEM),
            pl.BlockSpec(memory_space=pltpu.VMEM),
        ),
        scratch_shapes=[
            pltpu.VMEM((local_rows, width // 2), jnp.bfloat16),
            pltpu.SemaphoreType.DMA,
            pltpu.SemaphoreType.DMA,
            pltpu.SemaphoreType.DMA((count // 2, CHUNKS)),
            pltpu.SemaphoreType.DMA((count, CHUNKS)),
            pltpu.SemaphoreType.DMA((count // 2, CHUNKS)),
        ],
        compiler_params=pltpu.CompilerParams(
            collective_id=0, has_side_effects=True, vmem_limit_bytes=60000 * 1024
        ),
    )(kv, queries)


def attend_kernel(
    heads, rows, tile,
    choice, meta, q_ref, gate_ref, store_ref, cw_ref, local_ref, out_ref,
    values_one, lead_sum, own_sum, comp_k, comp_v, sel_k, sel_v, win_k, win_v,
):
    step = pl.program_id(0)
    position = meta[0]
    seq_len = meta[1]
    width = q_ref.shape[1]
    comp_total = comp_k.shape[0]

    @pl.when(step == 0)
    def _():
        live = (position + 1) * rows
        lead_sum[...] = jnp.zeros_like(lead_sum)
        own_sum[...] = jnp.zeros_like(own_sum)
        span = 16 * STRIDE
        first = jnp.concatenate([cw_ref[0, :STRIDE], cw_ref[1, :STRIDE]], axis=1)
        second = jnp.concatenate([cw_ref[0, STRIDE:], cw_ref[1, STRIDE:]], axis=1)

        def summarize(index, _):
            at = pl.ds(pl.multiple_of(index * span, span), span)
            both = store_ref[at, :]
            values_one[at, :width] = both[:, width:]
            values_one[at, width:] = jnp.ones((span, width), jnp.bfloat16)
            wide = both.astype(jnp.float32).reshape(16, STRIDE, 2 * width)
            lead_sum[pl.ds(pl.multiple_of(index * 16 + 8, 8), 16), :] = jnp.sum(
                wide * first[None], axis=1
            )
            own_sum[pl.ds(pl.multiple_of(index * 16, 16), 16), :] = jnp.sum(
                wide * second[None], axis=1
            )
            return 0

        lax.fori_loop(0, live // span, summarize, 0)
        merged = (lead_sum[7 : 7 + comp_total, :] + own_sum[...]).astype(jnp.bfloat16)
        known = lax.broadcasted_iota(jnp.int32, merged.shape, 0) < live // STRIDE
        merged = jnp.where(known, merged, jnp.zeros_like(merged))
        comp_k[...] = merged[:, :width]
        comp_v[:, :width] = merged[:, width:]
        comp_v[:, width:] = jnp.ones((comp_total, width), jnp.bfloat16)

    start = position * rows + step * SBLK

    @pl.when(start >= seq_len)
    def _():
        out_ref[...] = jnp.zeros_like(out_ref)

    def run(local):
        block = position * (rows // SBLK) + step
        half = lax.rem(step, 2) * SBLK
        base = start - half
        count = jnp.int32(0)
        for k in range(NSEL):
            count = count + (choice[step * NSEL + k] <= block).astype(jnp.int32)
        others = count - 1
        anchor = store_ref[pl.ds(pl.multiple_of(start, SBLK), 16), :width][:1]

        def place(k_out, v_out, target, source, length, valid):
            at = pl.ds(pl.multiple_of(source, SBLK), length)
            rows_at = slice(target, target + length)
            held = values_one[at, :]
            k_out[rows_at, :] = jnp.where(valid, store_ref[at, :width], anchor)
            v_out[rows_at, :] = jnp.where(valid, held, jnp.zeros_like(held))

        for k in range(NSEL):
            if k == NSEL - 1:
                picked = block
            else:
                picked = choice[step * NSEL + k + (k >= others).astype(jnp.int32)]
            valid = (k < others) | (k == NSEL - 1)
            place(sel_k, sel_v, k * SBLK, picked * SBLK, SBLK, valid)
        for k in range(0 if local else WIN // PAIR):
            source = base - (WIN - PAIR) + k * PAIR
            place(win_k, win_v, k * PAIR, jnp.maximum(source, 0), PAIR, source >= 0)
        if not local:
            place(win_k, win_v, WIN, jnp.maximum(base - WIN, 0), PAIR, base >= WIN)

        def col_of(n):
            return lax.broadcasted_iota(jnp.int32, (1, n), 1)

        early = (NSEL - 2) * SBLK
        late_col = col_of(PAIR)
        late_from = jnp.where(late_col < SBLK, -1, late_col - SBLK)
        comp_end = col_of(comp_total) * STRIDE + (STRIDE - 1)

        for part in range(SBLK * heads // tile):
            at = slice(part * tile, (part + 1) * tile)
            q = q_ref[at, :]
            q_both = split_scaled(q)
            row = (
                lax.broadcasted_iota(jnp.int32, (tile, 1), 0) + part * tile
            ) // heads
            token = row + start

            scores = dot_both(q_both, comp_k[...])
            scores = jnp.where(comp_end <= token, scores, NEGATIVE)
            compressed = finish(weigh(scores), comp_v[...])
            compressed = jnp.where(token >= STRIDE - 1, compressed, 0.0)

            scores = dot_both(q_both, sel_k[...])
            scores = jnp.concatenate(
                [
                    scores[:, :early],
                    jnp.where(late_from <= row, scores[:, early:], NEGATIVE),
                ],
                axis=1,
            )
            selected = finish(weigh(scores), sel_v[...])

            if local:
                window = local_ref[at, :].astype(jnp.float32)
            else:
                window = window_of(q_both, win_k[...], win_v[...], late_col <= row + half)

            wide = q.astype(jnp.float32).reshape(tile // heads, heads, width)
            gates = [
                jax.nn.sigmoid(
                    jnp.sum(
                        (wide * gate_ref[k].astype(jnp.float32)[None]).reshape(tile, width),
                        axis=1,
                        keepdims=True,
                    )
                )
                for k in range(3)
            ]
            combined = gates[0] * compressed + gates[1] * selected + gates[2] * window
            out_ref[at, :] = jnp.where(token < seq_len, combined, 0.0).astype(jnp.bfloat16)

    far = WIN // SBLK

    @pl.when((start < seq_len) & (step < far))
    def _():
        run(False)

    @pl.when((start < seq_len) & (step >= far))
    def _():
        run(True)


def attend(queries, gate_weight, store, compress_weight, choice, meta, local, rows):
    total_rows, width = queries.shape
    heads = gate_weight.shape[1]
    block_rows = SBLK * heads
    tile = min(1024, block_rows)
    tokens = store.shape[0]
    comp_total = tokens // STRIDE
    whole = pl.BlockSpec(memory_space=pltpu.VMEM)
    return pl.pallas_call(
        functools.partial(attend_kernel, heads, rows, tile),
        grid_spec=pltpu.PrefetchScalarGridSpec(
            num_scalar_prefetch=2,
            grid=(rows // SBLK,),
            in_specs=[
                pl.BlockSpec((block_rows, width), lambda i, *_: (i, 0)),
                whole,
                whole,
                whole,
                pl.BlockSpec(
                    (block_rows, width),
                    lambda i, *_: (jnp.maximum(i - WIN // SBLK, 0), 0),
                ),
            ],
            out_specs=pl.BlockSpec((block_rows, width), lambda i, *_: (i, 0)),
            scratch_shapes=[
                pltpu.VMEM((tokens, 2 * width), jnp.bfloat16),
                pltpu.VMEM((comp_total + 8, 2 * width), jnp.float32),
                pltpu.VMEM((comp_total, 2 * width), jnp.float32),
                pltpu.VMEM((comp_total, width), jnp.bfloat16),
                pltpu.VMEM((comp_total, 2 * width), jnp.bfloat16),
                pltpu.VMEM((NSEL * SBLK, width), jnp.bfloat16),
                pltpu.VMEM((NSEL * SBLK, 2 * width), jnp.bfloat16),
                pltpu.VMEM((WIN + PAIR, width), jnp.bfloat16),
                pltpu.VMEM((WIN + PAIR, 2 * width), jnp.bfloat16),
            ],
        ),
        out_shape=jax.ShapeDtypeStruct((total_rows, width), jnp.bfloat16),
        compiler_params=pltpu.CompilerParams(
            dimension_semantics=("arbitrary",), vmem_limit_bytes=60000 * 1024
        ),
    )(choice, meta, queries, gate_weight, store, compress_weight, local)


def per_device(queries, keys, values, compress_weight, gate_weight, selection, seq_len):
    rows, heads, width = queries.shape
    count = lax.axis_size("ctx")
    position = lax.axis_index("ctx")
    group = lax.axis_index("head") * heads // (H // G)
    key_mine = lax.dynamic_index_in_dim(keys, group, 1, keepdims=False)
    value_mine = lax.dynamic_index_in_dim(values, group, 1, keepdims=False)
    kv = jnp.concatenate([key_mine, value_mine], axis=1)
    flat = queries.reshape(rows * heads, width)
    store, local = share(kv, flat, count, heads)
    per_dev = rows // SBLK
    choice = lax.dynamic_slice(
        selection, (position * per_dev, group, 0), (per_dev, 1, NSEL)
    ).reshape(-1)
    meta = jnp.stack([position.astype(jnp.int32), seq_len[0]])
    out = attend(
        flat, gate_weight, store, compress_weight, choice, meta, local, rows,
    )
    return out.reshape(rows, heads, width)


def solution(mesh):
    return jax.shard_map(
        per_device,
        mesh=mesh,
        in_specs=(
            P(("grp", "ctx"), "head", None),
            P(("grp", "ctx"), None, None),
            P(("grp", "ctx"), None, None),
            P(),
            P(None, "head", None),
            P("grp", None, None),
            P("grp"),
        ),
        out_specs=P(("grp", "ctx"), "head", None),
        check_vma=False,
    )
```
